32 devices in a mesh: samp: 4 (over y, x), box: 8 (over z, core).
Axes of the slice: x: 2, y: 2, z: 4, core: 2. Of those that a mesh axis runs over, the one named last changes fastest.
Arguments:
- pattern_a: float32 [1024, 2, 18432], P('box', None, 'samp'), may hold values from -6 to 6
- children_b: int32 [256, 8], P('box'), may hold values from -1 to 1023, as said below
- children_c: int32 [64, 8], P('box'), may hold values from -1 to 255, as said below
- theta_ab: float32 [96, 128], replicated, may hold values from -0.625 to 0.625
- theta_bc: float32 [128, 160], replicated, may hold values from -0.5 to 0.5
- phi_start_b: int32 [256], P('samp'), may hold values from 0 to 191, as said below
- phi_weight_b: float32 [4, 256], P(None, 'samp'), may hold values from -0.25 to 1
- phi_start_c: int32 [320], P('samp'), may hold values from 0 to 255, as said below
- phi_weight_c: float32 [4, 320], P(None, 'samp'), may hold values from -0.25 to 1
- translation: float32 [316, 2, 51200], P(None, None, 'samp'), may hold values from -0.1875 to 0.1875
- list_src: int32 [64, 32], P('box'), may hold values from 0 to 63
- list_vec: int32 [64, 32], P('box'), may hold values from 0 to 315
Outputs:
- incoming: float32 [64, 2, 51200], P('box', None, 'samp')
The draws below stay inside these ranges and needn't reach their ends.
Inputs may be any that keep to these rules, and one draw needn't show every extreme that they name: `children_b`: entry o of a row is -1 or the level-A box in octant o = 4 ox + 2 oy + oz of that level-B box; level-B box p and its children lie on the same index of box, boxes p // 32 and c // 128 being equal; every level-A box is the child of exactly one level-B box. `children_c`: entry o of a row is -1 or the level-B box in octant o of that level-C box; p // 8 equals c // 32; every level-B box is the child of exactly one level-C box. phi_start_b[m] is (m * 192 // 256 - 1) or (m * 192 // 256 - 2), modulo 192. phi_start_c[m] is (m * 256 // 320 - 1) or (m * 256 // 320 - 2), modulo 256.
All inputs are finite; a program needn't handle non-finite values.
Results may differ from the reference program's by a relative error of at most 0.000071.
Values sent between devices are 32-bit elements; how exact they have to be, the bound alone decides.
A program may use at most 192 MiB of HBM per device.

```python
import jax
import jax.numpy as jnp
from jax import lax

THETA_A = 96
PHI_A = 192
THETA_B = 128
PHI_B = 256
THETA_C = 160
PHI_C = 320
SIZE_B = 8
SIZE_C = 16
LIST = 32
VECTORS = 316
BC_DEV = 8
BB_DEV = 32
BA_DEV = 128
NBA = 1024
NBB = 256
NBC = 64


def octree_slots(key, parents_dev, children_dev, parents_all):

    def one_block(block_id):
        ranking = jax.random.permutation(jax.random.fold_in(key, block_id), 8 * parents_dev).astype(jnp.int32)
        return jnp.where(ranking < children_dev, ranking + block_id * children_dev, -1).reshape(parents_dev, 8)
    block_ids = jnp.arange(parents_all // parents_dev, dtype=jnp.int32)
    blocks = jax.vmap(one_block)(block_ids)
    return blocks.reshape(parents_all, 8).astype(jnp.int32)


def stencil_starts(key, n_parent, n_child):
    parent_ids = jnp.arange(n_parent, dtype=jnp.int32)
    nearest = parent_ids * n_child // n_parent
    backoff = jax.random.randint(key, (n_parent,), 1, 3, dtype=jnp.int32)
    return ((nearest - backoff) % n_child).astype(jnp.int32)


def draw_children_b(key, part):
    return octree_slots(jax.random.fold_in(key, 101), BB_DEV, BA_DEV, NBB)


def draw_children_c(key, part):
    return octree_slots(jax.random.fold_in(key, 202), BC_DEV, BB_DEV, NBC)


def draw_phi_start_b(key, part):
    return stencil_starts(jax.random.fold_in(key, 303), PHI_B, PHI_A)


def draw_phi_start_c(key, part):
    return stencil_starts(jax.random.fold_in(key, 404), PHI_C, PHI_B)


def plant(drawn, stream_key, low, largest):
    shape = drawn.shape
    spot = [jax.random.randint(jax.random.fold_in(stream_key, axis), (), 0, shape[axis]) for axis in range(len(shape))]
    drawn = drawn.at[tuple(spot)].set(low)
    longest = shape.index(max(shape))
    spot[longest] = (spot[longest] + 1) % shape[longest]
    return drawn.at[tuple(spot)].set(largest)


def level_of(rng, dims, shards, low, largest):
    factor_of = 1.0
    for position, shards_of in shards:
        draws = jax.random.uniform(jax.random.fold_in(jax.random.fold_in(rng, 6), position), (shards_of,), jnp.float32, low / len(shards), largest / len(shards))
        factor_of = factor_of * jnp.repeat(jnp.exp(draws), dims[position] // shards_of).reshape((-1,) + (1,) * (len(dims) - 1 - position))
    return factor_of


def noise(key, extent, width, bound, pieces=(), kind=jnp.bfloat16):
    gain = level_of(key, extent, pieces, -0.22, 0.18) if pieces else 1.0
    array = jax.random.normal(key, extent, jnp.float32) * width * gain
    return jnp.minimum(jnp.maximum(array, -bound), bound).astype(kind)


def setup_inputs(seed: int = 0) -> dict:
    arg_keys = jax.random.split(jax.random.key(seed), 13)
    pattern_a = noise(arg_keys[0], (NBA, 2, PHI_A * THETA_A), 1.0, 6.0, ((0, 8), (2, 4)), jnp.float32)
    children_b = draw_children_b(jax.random.fold_in(arg_keys[12], 71), 0)
    children_c = draw_children_c(jax.random.fold_in(arg_keys[12], 71), 0)
    theta_ab = noise(arg_keys[3], (THETA_A, THETA_B), THETA_A ** -0.5, 0.625, (), jnp.float32)
    theta_bc = noise(arg_keys[4], (THETA_B, THETA_C), THETA_B ** -0.5, 0.5, (), jnp.float32)
    phi_start_b = draw_phi_start_b(jax.random.fold_in(arg_keys[12], 71), 0)
    phi_weight_b = jnp.clip(-0.25 + 1.25 * jax.random.uniform(arg_keys[6], (4, PHI_B), jnp.float32) ** level_of(arg_keys[6], (4, PHI_B), ((1, 4),), -0.2, 0.2), -0.25, 1.0)
    phi_start_c = draw_phi_start_c(jax.random.fold_in(arg_keys[12], 71), 0)
    phi_weight_c = jnp.clip(-0.25 + 1.25 * jax.random.uniform(arg_keys[8], (4, PHI_C), jnp.float32) ** level_of(arg_keys[8], (4, PHI_C), ((1, 4),), -0.2, 0.2), -0.25, 1.0)
    translation = noise(arg_keys[9], (VECTORS, 2, PHI_C * THETA_C), 0.03, 0.1875, ((2, 4),), jnp.float32)
    list_src = plant(jax.random.randint(arg_keys[10], (NBC, LIST), 0, NBC), jax.random.fold_in(arg_keys[10], 1), 0, NBC - 1).astype(jnp.int32)
    list_vec = plant(jax.random.randint(arg_keys[11], (NBC, LIST), 0, VECTORS), jax.random.fold_in(arg_keys[11], 1), 0, VECTORS - 1).astype(jnp.int32)
    return dict(pattern_a=pattern_a, children_b=children_b, children_c=children_c, theta_ab=theta_ab, theta_bc=theta_bc, phi_start_b=phi_start_b, phi_weight_b=phi_weight_b, phi_start_c=phi_start_c, phi_weight_c=phi_weight_c, translation=translation, list_src=list_src, list_vec=list_vec)


PRECISE = lax.Precision.HIGHEST


def directions(n_theta, n_phi, phi_first, phi_count):
    polar = jnp.pi * (jnp.arange(n_theta, dtype=jnp.int32).astype(jnp.float32) + 0.5) / n_theta
    azimuth = 2.0 * jnp.pi * (phi_first + jnp.arange(phi_count, dtype=jnp.int32)).astype(jnp.float32) / n_phi
    polar_sine = jnp.sin(polar)[None, :]
    dir_x = jnp.cos(azimuth)[:, None] * polar_sine
    dir_y = jnp.sin(azimuth)[:, None] * polar_sine
    dir_z = jnp.broadcast_to(jnp.cos(polar)[None, :], dir_x.shape)
    return dir_x, dir_y, dir_z


def aggregate(level, children, first_box, box_size, n_phi, phi_first):
    box_count = level.shape[0]
    flat = level.reshape(box_count, 2, level.shape[2] * level.shape[3])
    dir_x, dir_y, dir_z = directions(level.shape[3], n_phi, phi_first, level.shape[2])
    summed = jnp.zeros((children.shape[0], 2, flat.shape[2]), jnp.float32)
    for octant in range(8):
        sign_x = 2.0 * ((octant >> 2) & 1) - 1.0
        sign_y = 2.0 * ((octant >> 1) & 1) - 1.0
        sign_z = 2.0 * (octant & 1) - 1.0
        phase = (0.5 * jnp.pi * box_size) * (sign_x * dir_x + sign_y * dir_y + sign_z * dir_z)
        cosine = jnp.cos(phase).reshape(-1)
        sine_part = jnp.sin(phase).reshape(-1)
        child_ids = (children[:, octant] - first_box).astype(jnp.int32)
        present = (children[:, octant] >= 0).astype(jnp.float32)[:, None]
        picked = jnp.take(flat, jnp.clip(child_ids, 0, box_count - 1), axis=0)
        real_part = picked[:, 0] * cosine - picked[:, 1] * sine_part
        imag_part = picked[:, 0] * sine_part + picked[:, 1] * cosine
        summed = summed + jnp.stack([present * real_part, present * imag_part], axis=1)
    return summed


def translate(rows, operators, vectors):
    picked = jnp.take(operators, vectors.reshape(-1), axis=0).reshape(rows.shape)
    real_part = jnp.sum(picked[:, :, 0] * rows[:, :, 0] - picked[:, :, 1] * rows[:, :, 1], axis=1)
    imag_part = jnp.sum(picked[:, :, 0] * rows[:, :, 1] + picked[:, :, 1] * rows[:, :, 0], axis=1)
    return jnp.stack([real_part, imag_part], axis=1)


def interpolate(pattern, theta_matrix, phi_start, phi_weight, n_phi_child, n_theta_child):
    box_count = pattern.shape[0]
    grid = pattern.reshape(box_count, 2, n_phi_child, n_theta_child)
    grid = jnp.einsum('bcpt,tu->bcpu', grid, theta_matrix, precision=PRECISE)
    summed = jnp.zeros((box_count, 2, phi_start.shape[0], theta_matrix.shape[1]), jnp.float32)
    for offset in range(4):
        cell_ids = ((phi_start + offset) % n_phi_child).astype(jnp.int32)
        summed = summed + phi_weight[offset][None, None, :, None] * jnp.take(grid, cell_ids, axis=2)
    return summed


def reference(pattern_a, children_b, children_c, theta_ab, theta_bc, phi_start_b, phi_weight_b, phi_start_c, phi_weight_c, translation, list_src, list_vec):
    level_b = interpolate(pattern_a, theta_ab, phi_start_b, phi_weight_b, PHI_A, THETA_A)
    pattern_b = aggregate(level_b, children_b, 0, SIZE_B, PHI_B, 0)
    level_c = interpolate(pattern_b, theta_bc, phi_start_c, phi_weight_c, PHI_B, THETA_B)
    pattern_c = aggregate(level_c, children_c, 0, SIZE_C, PHI_C, 0)

    def one_target(entry):
        sources, vectors = entry
        rows = jnp.take(pattern_c, sources, axis=0)[None]
        return translate(rows, translation, vectors[None])[0]

    return lax.map(one_target, (list_src, list_vec))
```

```python
import functools
import math

import jax
import jax.numpy as jnp
import numpy as np
from jax import lax
from jax.experimental import pallas as pl
from jax.experimental.pallas import tpu as pltpu
from jax.sharding import PartitionSpec as P

SIZE_B = 8
SIZE_C = 16
LANES = 128
GROUP = 4


def window(first, last, n_child, n_parent):
    low = 0
    while (low - 1) * n_child // n_parent + 2 >= first:
        low -= 1
    high = 0
    while (high + 1) * n_child // n_parent - 2 <= last:
        high += 1
    return low, high + 1


def phase_table(parts, per_part, low, high, n_theta, size):
    n_phi = parts * per_part
    theta = np.pi * (np.arange(n_theta) + 0.5) / n_theta
    first = np.arange(parts)[:, None] * per_part
    phi = 2.0 * np.pi * (first + np.arange(low, high)[None]) / n_phi
    u_x = np.cos(phi)[..., None] * np.sin(theta)
    u_y = np.sin(phi)[..., None] * np.sin(theta)
    u_z = np.broadcast_to(np.cos(theta), u_x.shape)
    psi = []
    for o in range(8):
        s_x, s_y, s_z = 2 * (o >> 2 & 1) - 1, 2 * (o >> 1 & 1) - 1, 2 * (o & 1) - 1
        psi.append(0.5 * np.pi * size * (s_x * u_x + s_y * u_y + s_z * u_z))
    psi = np.stack(psi, axis=2)
    return np.concatenate([np.cos(psi), np.sin(psi)], axis=2).astype(np.float32)


def split(x):
    high = x.astype(jnp.bfloat16)
    return high, (x - high.astype(jnp.float32)).astype(jnp.bfloat16)


def split_outside(x):
    high = lax.reduce_precision(x, exponent_bits=8, mantissa_bits=7)
    return high.astype(jnp.bfloat16), (x - high).astype(jnp.bfloat16)


def mm(a, b):
    return jnp.dot(a, b, preferred_element_type=jnp.float32)


def aggregate_kernel(
    steps, az_step, wb, wc, out_rows,
    samp, idx_b, wgt_b, idx_c, wgt_c,
    x_ref, tab_ref, sb_ref, phb_ref, tbc_ref, sc_ref, phc_ref,
    o_ref, grid_a, grid_b,
):
    step = pl.program_id(0)
    count_a = x_ref.shape[0]
    rows_x = x_ref.shape[1]
    rows = x_ref.reshape(count_a * rows_x, LANES)
    for c in range(2):
        for q in range(az_step // GROUP):
            tiles = [
                split(rows[pl.ds(6 * q + 2 * j + c, count_a, stride=rows_x), :]) for j in range(3)
            ]
            for pair in range(2):
                high = jnp.concatenate([tiles[pair][0], tiles[pair + 1][0]], axis=1)
                low = jnp.concatenate([tiles[pair][1], tiles[pair + 1][1]], axis=1)
                both = mm(high, tab_ref[pair, 0]) + mm(low, tab_ref[pair, 0]) + mm(high, tab_ref[pair, 1])
                for k in range(2):
                    place = step * az_step + q * GROUP + pair * 2 + k
                    grid_a[place, c * count_a : (c + 1) * count_a, :] = both[:, k * LANES : (k + 1) * LANES]

    @pl.when(step == steps - 1)
    def _():
        count_b = sb_ref.shape[0] // 8
        n_theta_c = tbc_ref.shape[2]

        def level_b(m, carry):
            parts = []
            for c in range(2):
                here = slice(c * count_a, (c + 1) * count_a)
                value = wgt_b[0, m] * grid_a[idx_b[0, m], here, :]
                for k in range(1, 4):
                    value = value + wgt_b[k, m] * grid_a[idx_b[k, m], here, :]
                parts.append(split(value))
            stacked = jnp.concatenate(
                [
                    jnp.concatenate([parts[0][0], parts[1][0]], axis=1),
                    jnp.concatenate([parts[0][1], parts[1][1]], axis=1),
                ],
                axis=0,
            )
            picked = mm(sb_ref[...], stacked)
            real = jnp.zeros((count_b, LANES), jnp.float32)
            imag = jnp.zeros((count_b, LANES), jnp.float32)
            for o in range(8):
                cosine = phb_ref[m, o : o + 1, :]
                sine = phb_ref[m, 8 + o : 9 + o, :]
                pr = picked[o * count_b : (o + 1) * count_b, :LANES]
                pi = picked[o * count_b : (o + 1) * count_b, LANES:]
                real = real + pr * cosine - pi * sine
                imag = imag + pr * sine + pi * cosine
            high, low = split(jnp.concatenate([real, imag], axis=0))
            both = jnp.concatenate([high, low], axis=1)
            grid_b[m] = mm(both, tbc_ref[0]) + mm(high, tbc_ref[1, :LANES])
            return carry

        lax.fori_loop(0, wb, level_b, 0)

        count_c = sc_ref.shape[0] // 8

        def level_c(g, carry):
            reals, imags = [], []
            for i in range(GROUP):
                n = g * GROUP + i
                value = wgt_c[0, n] * grid_b[idx_c[0, n]]
                for k in range(1, 4):
                    value = value + wgt_c[k, n] * grid_b[idx_c[k, n]]
                high, low = split(value)
                rr = mm(sc_ref[...], jnp.concatenate([high[:count_b], low[:count_b]], axis=0))
                ri = mm(sc_ref[...], jnp.concatenate([high[count_b:], low[count_b:]], axis=0))
                real = jnp.zeros((count_c, n_theta_c), jnp.float32)
                imag = jnp.zeros((count_c, n_theta_c), jnp.float32)
                for o in range(8):
                    cosine = phc_ref[n, o : o + 1, :]
                    sine = phc_ref[n, 8 + o : 9 + o, :]
                    pr = rr[o * count_c : (o + 1) * count_c]
                    pi = ri[o * count_c : (o + 1) * count_c]
                    real = real + pr * cosine - pi * sine
                    imag = imag + pr * sine + pi * cosine
                reals.append(real)
                imags.append(imag)
            for c, flat in enumerate((jnp.concatenate(reals, axis=1), jnp.concatenate(imags, axis=1))):
                tiles = flat.shape[1] // LANES
                for t in range(tiles):
                    o_ref[pl.ds(g * 2 * tiles + 2 * t + c, count_c, stride=out_rows), :] = flat[
                        :, t * LANES : (t + 1) * LANES
                    ]
            return carry

        lax.fori_loop(0, wc // GROUP, level_c, 0)


def translate_kernel(list_len, chunk, src, vec, x_ref, t_hbm, o_ref, real, imag, buf, sem):
    p = pl.program_id(0)
    count = pl.num_programs(0)
    n_src, samples = x_ref.shape[0], x_ref.shape[2]
    slot = lax.rem(p, 2)

    def fetch(target, where):
        def one(l, carry):
            pltpu.make_async_copy(
                t_hbm.at[vec[target * list_len + l]], buf.at[where, l], sem.at[where]
            ).start()
            return carry

        lax.fori_loop(0, list_len, one, 0)

    @pl.when(p == 0)
    def _():
        fetch(0, 0)

    @pl.when(p + 1 < count)
    def _():
        fetch(p + 1, 1 - slot)

    @pl.when(p == 0)
    def _():
        def one(s, carry):
            for r in range(0, samples, chunk):
                here = slice(r, r + chunk)
                real[s, :, here] = jnp.broadcast_to(x_ref[s, 0:1, here], (2, chunk))
                imag[s, :, here] = jnp.broadcast_to(x_ref[s, 1:2, here], (2, chunk))
            return carry

        lax.fori_loop(0, n_src, one, 0)

    def drain(l, carry):
        pltpu.make_async_copy(t_hbm.at[0], buf.at[slot, l], sem.at[slot]).wait()
        return carry

    lax.fori_loop(0, list_len, drain, 0)

    def one_chunk(i, carry):
        r = pl.ds(pl.multiple_of(i * chunk, chunk), chunk)
        by_real = jnp.zeros((2, chunk), jnp.float32)
        by_imag = jnp.zeros((2, chunk), jnp.float32)
        for l in range(list_len):
            s = src[p * list_len + l]
            t = buf[slot, l, :, r]
            by_real = by_real + t * real[s, :, r]
            by_imag = by_imag + t * imag[s, :, r]
        o_ref[0, 0:1, r] = by_real[0:1] - by_imag[1:2]
        o_ref[0, 1:2, r] = by_imag[0:1] + by_real[1:2]
        return carry

    lax.fori_loop(0, samples // chunk, one_chunk, 0)


def pick_chunk(samples):
    for tiles in (20, 16, 12, 8, 4, 2, 1):
        if samples % (tiles * LANES) == 0:
            return tiles * LANES
    return samples


def interleave(x):
    return x.reshape(x.shape[0], 2, -1, LANES).transpose(0, 2, 1, 3).reshape(x.shape[0], -1, LANES)


def stencil(start, weight, first, low, high, src_low, src_high, n_child):
    nearest = start - first
    tap = nearest[None, :] + jnp.arange(4, dtype=jnp.int32)[:, None]
    half = n_child // 2
    tap = (tap + half) % n_child - half
    centre = (src_low + src_high) // 2
    tap = jnp.where(tap - centre > half, tap - n_child, tap)
    tap = jnp.where(tap - centre < -half, tap + n_child, tap)
    inside = (tap >= src_low) & (tap < src_high)
    rows = jnp.clip(tap - src_low, 0, src_high - src_low - 1)
    return rows.astype(jnp.int32), jnp.where(inside, weight, 0.0)


def one_hot(children, first, count):
    ids = (children - first).T.reshape(-1)
    hot = ((ids[:, None] == jnp.arange(count)[None, :]) & (children.T.reshape(-1) >= 0)[:, None]).astype(jnp.bfloat16)
    return jnp.concatenate([hot, hot], axis=1)


def per_device(
    n_samp,
    pattern_a, children_b, children_c, theta_ab, theta_bc,
    phi_start_b, phi_weight_b, phi_start_c, phi_weight_c,
    translation, list_src, list_vec,
):
    samp = lax.axis_index("samp")
    box = lax.axis_index("box")
    count_a, count_b, count_c = pattern_a.shape[0], children_b.shape[0], children_c.shape[0]
    theta_a, theta_b = theta_ab.shape
    theta_c = theta_bc.shape[1]
    pa = pattern_a.shape[2] // theta_a
    pb = phi_start_b.shape[0]
    pc = phi_start_c.shape[0]
    n_a, n_b, n_c = n_samp * pa, n_samp * pb, n_samp * pc
    low_b, high_b = window(0, pa - 1, n_a, n_b)
    low_c, high_c = window(low_b, high_b - 1, n_b, n_c)
    ext = -(-max(-low_c, high_c - pc) // GROUP) * GROUP
    low_c, high_c = -ext, pc + ext
    wb, wc = high_b - low_b, high_c - low_c

    up = [(i, (i + 1) % n_samp) for i in range(n_samp)]
    down = [((i + 1) % n_samp, i) for i in range(n_samp)]
    table_b = jnp.concatenate([phi_start_b.astype(jnp.float32)[None], phi_weight_b], axis=0)
    table_c = jnp.concatenate([phi_start_c.astype(jnp.float32)[None], phi_weight_c], axis=0)
    near = max(ext, -low_b, high_b - pb)
    left = lax.ppermute(jnp.concatenate([table_b[:, pb - near :], table_c[:, pc - near :]], 1), "samp", up)
    right = lax.ppermute(jnp.concatenate([table_b[:, :near], table_c[:, :near]], 1), "samp", down)
    table_b = jnp.concatenate([left[:, near + low_b : near], table_b, right[:, : high_b - pb]], 1)
    table_c = jnp.concatenate([left[:, 2 * near - ext :], table_c, right[:, near : near + ext]], 1)
    idx_b, wgt_b = stencil(
        table_b[0].astype(jnp.int32), table_b[1:], samp * pa, low_b, high_b, 0, pa, n_a
    )
    idx_c, wgt_c = stencil(
        table_c[0].astype(jnp.int32), table_c[1:], samp * pb, low_c, high_c, low_b, high_b, n_b
    )

    tab = []
    for pair in range(2):
        at = pair * (2 * theta_a - LANES)
        blocks = jnp.zeros((2 * LANES, 2 * theta_b), jnp.float32)
        for k in range(2):
            blocks = lax.dynamic_update_slice(blocks, theta_ab, (at + k * theta_a, k * theta_b))
        tab.append(jnp.stack(split_outside(blocks)))
    tab = jnp.stack(tab)
    high, low = split_outside(theta_bc)
    tbc = jnp.stack([jnp.concatenate([high, high], 0), jnp.concatenate([low, low], 0)])
    s_b = one_hot(children_b, box * count_a, count_a)
    s_c = one_hot(children_c, box * count_b, count_b)
    phb = jnp.asarray(phase_table(n_samp, pb, low_b, high_b, theta_b, SIZE_B))
    phc = jnp.asarray(phase_table(n_samp, pc, low_c, high_c, theta_c, SIZE_C))

    x = interleave(pattern_a)
    steps = pa // 16 if pa % 16 == 0 else 1
    x = jnp.pad(x, ((0, 0), (0, -x.shape[1] % 8), (0, 0)))
    rows_x = x.shape[1]
    az_step = pa // steps
    tiles = GROUP * theta_c // LANES
    out_rows = wc // GROUP * 2 * tiles
    ext_rows = ext // GROUP * 2 * tiles
    rows = pc // GROUP * 2 * tiles
    one = pl.Buffered(1)
    wide = pl.pallas_call(
        functools.partial(aggregate_kernel, steps, az_step, wb, wc, out_rows),
        grid_spec=pltpu.PrefetchScalarGridSpec(
            num_scalar_prefetch=5,
            grid=(steps,),
            in_specs=[
                pl.BlockSpec((count_a, rows_x // steps, LANES), lambda i, *_: (0, i, 0)),
                pl.BlockSpec(tab.shape, lambda i, *_: (0, 0, 0, 0), pipeline_mode=one),
                pl.BlockSpec(s_b.shape, lambda i, *_: (0, 0), pipeline_mode=one),
                pl.BlockSpec((None,) + phb.shape[1:], lambda i, s, *_: (s[0], 0, 0, 0), pipeline_mode=one),
                pl.BlockSpec(tbc.shape, lambda i, *_: (0, 0, 0), pipeline_mode=one),
                pl.BlockSpec(s_c.shape, lambda i, *_: (0, 0), pipeline_mode=one),
                pl.BlockSpec((None,) + phc.shape[1:], lambda i, s, *_: (s[0], 0, 0, 0), pipeline_mode=one),
            ],
            out_specs=pl.BlockSpec((count_c * out_rows, LANES), lambda i, *_: (0, 0)),
            scratch_shapes=[
                pltpu.VMEM((pa, 2 * count_a, LANES), jnp.float32),
                pltpu.VMEM((wb, 2 * count_b, theta_c), jnp.float32),
            ],
        ),
        out_shape=jax.ShapeDtypeStruct((count_c * out_rows, LANES), jnp.float32),
        compiler_params=pltpu.CompilerParams(vmem_limit_bytes=48 << 20),
        name="aggregate",
    )(samp.reshape(1), idx_b, wgt_b, idx_c, wgt_c, x, tab, s_b, phb, tbc, s_c, phc)
    wide = wide.reshape(count_c, out_rows, LANES)
    from_left = lax.ppermute(wide[:, out_rows - ext_rows :], "samp", up)
    from_right = lax.ppermute(wide[:, :ext_rows], "samp", down)
    zeros = jnp.zeros((count_c, rows - ext_rows, LANES), jnp.float32)
    mine = (
        wide[:, ext_rows : out_rows - ext_rows]
        + jnp.concatenate([from_left, zeros], 1)
        + jnp.concatenate([zeros, from_right], 1)
    )
    mine = mine.reshape(count_c, rows // 2, 2, LANES).transpose(0, 2, 1, 3).reshape(count_c, 2, -1)
    everyone = lax.all_gather(mine, "box", axis=0, tiled=True)

    list_len = list_src.shape[1]
    n_src, _, samples = everyone.shape
    chunk = pick_chunk(samples)
    return pl.pallas_call(
        functools.partial(translate_kernel, list_len, chunk),
        grid_spec=pltpu.PrefetchScalarGridSpec(
            num_scalar_prefetch=2,
            grid=(count_c,),
            in_specs=[
                pl.BlockSpec(everyone.shape, lambda i, *_: (0, 0, 0), pipeline_mode=one),
                pl.BlockSpec(memory_space=pl.ANY),
            ],
            out_specs=pl.BlockSpec((1, 2, samples), lambda i, *_: (i, 0, 0)),
            scratch_shapes=[
                pltpu.VMEM(everyone.shape, jnp.float32),
                pltpu.VMEM(everyone.shape, jnp.float32),
                pltpu.VMEM((2, list_len, 2, samples), jnp.float32),
                pltpu.SemaphoreType.DMA((2,)),
            ],
        ),
        out_shape=jax.ShapeDtypeStruct((count_c, 2, samples), jnp.float32),
        compiler_params=pltpu.CompilerParams(vmem_limit_bytes=48 << 20),
        name="translate",
    )(list_src.reshape(-1), list_vec.reshape(-1), everyone, translation)


def solution(mesh):
    placed = (
        P("box", None, "samp"),
        P("box", None),
        P("box", None),
        P(),
        P(),
        P("samp"),
        P(None, "samp"),
        P("samp"),
        P(None, "samp"),
        P(None, None, "samp"),
        P("box", None),
        P("box", None),
    )
    return jax.shard_map(
        functools.partial(per_device, mesh.shape["samp"]),
        mesh=mesh, in_specs=placed, out_specs=P("box", None, "samp"), check_vma=False,
    )
```
